512 devices in a mesh: seq: 64 (over z, y), fsdp: 8 (over x, core).
Axes of the slice: x: 4, y: 8, z: 8, core: 2. Of those that a mesh axis runs over, the one named last changes fastest.
Arguments:
- query: bfloat16 [32768, 4096], P('seq', 'fsdp'), may hold values from -6 to 6
- key: bfloat16 [32768, 4096], P('seq', 'fsdp'), may hold values from -6 to 6
- value: bfloat16 [32768, 4096], P('seq', 'fsdp'), may hold values from -16 to 16, as said below
- cotangent: bfloat16 [32768, 4096], P('seq', 'fsdp'), may hold values from -16 to 16
- gain: float32 [4096], P('fsdp'), may hold values from 0.1 to 1.9
Outputs:
- query_grad: bfloat16 [32768, 4096], P('seq', 'fsdp')
- key_grad: bfloat16 [32768, 4096], P('seq', 'fsdp')
- value_grad: bfloat16 [32768, 4096], P('seq', 'fsdp')
- gain_grad: float32 [4096], P('fsdp')
The draws below stay inside these ranges and needn't reach their ends.
Inputs may be any that keep to these rules, and one draw needn't show every extreme that they name: `value`: values whose typical size differs from head to head.
All inputs are finite; a program needn't handle non-finite values.
Results may differ from the reference program's by a relative error of at most 0.0057.
Values sent between devices are 32-bit elements; how exact they have to be, the bound alone decides.
No kernel may reach another device: no remote copies, remote signals or barrier semaphores. Data moves between devices by JAX's collectives and lax.ppermute only.
A program may use at most 64 MiB of HBM per device.

```python
import math
import jax
import jax.numpy as jnp
from jax import lax

HEADS = 32
HEAD_DIM = 128
TOK_DEV = 512
HD = 4096
LENGTH = 32768


def draw_value(key, part):
    head = (jnp.arange(HD) // HEAD_DIM).astype(jnp.float32)
    rising = jnp.exp(math.log(3.0) * head / max(HEADS - 1, 1))
    noise = jnp.clip(jax.random.normal(jax.random.fold_in(key, 1), (LENGTH, HD), jnp.float32), -4.0, 4.0)
    return (noise * rising[None, :]).astype(jnp.bfloat16)


def spiked(result, rng, source, target, blocks, factor):
    def block_of(position):
        return (jnp.arange(result.shape[position]) // (result.shape[position] // blocks)).reshape((-1,) + (1,) * (result.ndim - 1 - position))

    near = jax.random.permutation(rng, blocks)[block_of(target)]
    second = (block_of(target) + blocks // 2) % blocks
    return jnp.where((block_of(source) == near) | (block_of(source) == second), factor * result, result)


def level_of(own_key, dims, pieces, low, top_value):
    factor_of, own = 1.0, jax.random.fold_in(own_key, 6)
    for dim, blocks in pieces:
        draws = jnp.exp(jax.random.uniform(jax.random.fold_in(own, dim), (blocks,), jnp.float32, low / len(pieces), top_value / len(pieces)))
        factor_of = factor_of * jnp.repeat(draws, dims[dim] // blocks).reshape([-1 if axis == dim else 1 for axis in range(len(dims))])
    return factor_of


def normal_values(key, extent, spread, most, shards=(), kind=jnp.bfloat16):
    result = jax.random.normal(key, extent, jnp.float32) * spread
    if len(shards) > 0:
        result = level_of(key, extent, shards, -0.22, 0.18) * result
    return jnp.clip(result, min=-most, max=most).astype(kind)


def bell_draw_with(key, shape, deviation, limit, pieces, heavy, kind=jnp.bfloat16):
    array = deviation * jax.random.normal(key, shape, jnp.float32)
    if pieces:
        array = array * level_of(key, shape, pieces, -0.22, 0.18)
    return jnp.clip(spiked(array, jax.random.fold_in(key, 3), *heavy), -limit, limit).astype(kind)


def setup_inputs(seed: int = 0) -> dict:
    key_of = jax.random.split(jax.random.key(seed), 6)
    query = normal_values(key_of[0], (LENGTH, HD), 1.0, 6.0, ((0, 64), (1, 8)))
    key = normal_values(key_of[1], (LENGTH, HD), 1.0, 6.0, ((0, 64), (1, 8)))
    value = draw_value(jax.random.fold_in(key_of[5], 71), 0)
    cotangent = bell_draw_with(key_of[3], (LENGTH, HD), 1.0, 16.0, ((0, 64), (1, 8)), (0, 1, 64, 4.0))
    gain = jnp.clip(1.0 + 0.18 * jax.random.normal(key_of[4], (HD,), jnp.float32), 0.1, 1.9)
    return {"query": query, "key": key, "value": value, "cotangent": cotangent, "gain": gain}


def block_state(items):
    left = items[0].astype(jnp.float32)
    right = items[1].astype(jnp.float32)
    return jnp.einsum('tha,thb->hab', left, right)

def reference(query, key, value, cotangent, gain):
    blocks = LENGTH // TOK_DEV
    shape = (blocks, TOK_DEV, HEADS, HEAD_DIM)
    qb = query.reshape(shape)
    kb = key.reshape(shape)
    vb = value.reshape(shape)
    causal = jnp.tril(jnp.ones((TOK_DEV, TOK_DEV), dtype=bool))
    states = lax.map(block_state, (kb, vb))
    zeros = jnp.zeros_like(states[:1])
    prefix = jnp.concatenate([zeros, jnp.cumsum(states, axis=0)[:-1]], axis=0)
    prefix_low = prefix.astype(jnp.bfloat16).astype(jnp.float32)

    def forward(items):
        qf = items[0].astype(jnp.float32)
        kf = items[1].astype(jnp.float32)
        vf = items[2].astype(jnp.float32)
        scores = jnp.einsum('tha,sha->hts', qf, kf)
        weights = jnp.where(causal[None], scores, 0.0).astype(jnp.bfloat16).astype(jnp.float32)
        out = jnp.einsum('hts,shb->thb', weights, vf) + jnp.einsum('tha,hab->thb', qf, items[3])
        return out.reshape(TOK_DEV, HD)
    attended = lax.map(forward, (qb, kb, vb, prefix_low)).reshape(LENGTH, HD)
    inv_rms = lax.rsqrt(lax.optimization_barrier(jnp.mean(attended * attended, axis=-1, keepdims=True)) + 1e-05)
    normed = attended * inv_rms
    upstream = cotangent.astype(jnp.float32)
    gain_grad = lax.optimization_barrier(jnp.sum(upstream * normed, axis=0)) * (1.0 / math.sqrt(LENGTH))
    scaled = upstream * gain
    attended_grad = (scaled - normed * lax.optimization_barrier(jnp.mean(scaled * normed, axis=-1, keepdims=True))) * inv_rms
    dof = attended_grad.astype(jnp.bfloat16).astype(jnp.float32).reshape(shape)
    grad_states = lax.map(block_state, (qb, dof))
    suffix = jnp.concatenate([jnp.cumsum(grad_states[::-1], axis=0)[::-1][1:], zeros], axis=0)
    suffix_low = suffix.astype(jnp.bfloat16).astype(jnp.float32)

    def backward(items):
        qf = items[0].astype(jnp.float32)
        kf = items[1].astype(jnp.float32)
        vf = items[2].astype(jnp.float32)
        grads = items[3]
        pre = items[4]
        suf = items[5]
        scores = jnp.einsum('tha,sha->hts', qf, kf)
        weights = jnp.where(causal[None], scores, 0.0).astype(jnp.bfloat16).astype(jnp.float32)
        score_grad = jnp.einsum('thb,shb->hts', grads, vf)
        score_grad = jnp.where(causal[None], score_grad, 0.0).astype(jnp.bfloat16).astype(jnp.float32)
        q_grad = jnp.einsum('hts,sha->tha', score_grad, kf) + jnp.einsum('thb,hab->tha', grads, pre)
        k_grad = jnp.einsum('hts,tha->sha', score_grad, qf) + jnp.einsum('shb,hab->sha', vf, suf)
        v_grad = jnp.einsum('hts,thb->shb', weights, grads) + jnp.einsum('sha,hab->shb', kf, suf)
        flat = (TOK_DEV, HD)
        return (q_grad.reshape(flat).astype(jnp.bfloat16), k_grad.reshape(flat).astype(jnp.bfloat16), v_grad.reshape(flat).astype(jnp.bfloat16))
    query_grad, key_grad, value_grad = lax.map(backward, (qb, kb, vb, dof, prefix_low, suffix_low))
    flat = (LENGTH, HD)
    return (query_grad.reshape(flat), key_grad.reshape(flat), value_grad.reshape(flat), gain_grad)
```

```python
import math

import jax
import jax.numpy as jnp
from jax import lax
from jax.experimental import pallas as pl
from jax.experimental.pallas import tpu as pltpu
from jax.sharding import PartitionSpec as P

HEAD_DIM = 128
HD = 4096
EPS = 1e-05
F32 = jnp.float32
BF16 = jnp.bfloat16
ROWS = 8
GAIN_ROWS = ROWS + 1


def dot(a, b, over_a, over_b):
    return lax.dot_general(a, b, (((over_a,), (over_b,)), ((), ())), preferred_element_type=F32)


def cols(h):
    return pl.ds(h * HEAD_DIM, HEAD_DIM)


def call(kernel, outs, flops, *args):
    out_bytes = sum(math.prod(o.shape) * o.dtype.itemsize for o in outs)
    in_bytes = sum(math.prod(a.shape) * a.dtype.itemsize for a in args)
    return pl.pallas_call(
        kernel,
        out_shape=tuple(outs),
        in_specs=[pl.BlockSpec(memory_space=pltpu.VMEM)] * len(args),
        out_specs=tuple(pl.BlockSpec(memory_space=pltpu.VMEM) for _ in outs),
        cost_estimate=pl.CostEstimate(
            flops=flops, transcendentals=0, bytes_accessed=in_bytes + out_bytes
        ),
        name=kernel.__name__,
    )(*args)


def state_kernel(k_ref, v_ref, out_ref):
    for h in range(k_ref.shape[1] // HEAD_DIM):
        out_ref[pl.ds(h * HEAD_DIM, HEAD_DIM), :] = dot(k_ref[:, cols(h)], v_ref[:, cols(h)], 0, 0)


def masked(scores, first_row, first_col):
    row = lax.broadcasted_iota(jnp.int32, scores.shape, 0) + first_row
    col = lax.broadcasted_iota(jnp.int32, scores.shape, 1) + first_col
    return jnp.where(row >= col, scores, 0.0)


def local_kernel(q_ref, k_ref, v_ref, weights_ref, local_ref):
    rows = q_ref.shape[0]
    block = min(256, rows)
    for h in range(q_ref.shape[1] // HEAD_DIM):
        for i in range(rows // block):
            mine = pl.ds(i * block, block)
            ends = (i + 1) * block
            scores = dot(q_ref[mine, cols(h)], k_ref[:ends, cols(h)], 1, 1)
            weights = masked(scores, i * block, 0).astype(BF16)
            weights_ref[h, mine, :ends] = weights
            local_ref[mine, cols(h)] = dot(weights, v_ref[:ends, cols(h)], 1, 0)


def prefix_kernel(in_ref, out_ref):
    acc = jnp.zeros(in_ref.shape[1:], F32)
    for j in range(in_ref.shape[0]):
        out_ref[j] = acc
        acc = acc + in_ref[j]


def suffix_kernel(in_ref, out_ref):
    count = in_ref.shape[0] // GAIN_ROWS
    acc = jnp.zeros((ROWS, HEAD_DIM), F32)
    gain = jnp.zeros((1, HEAD_DIM), F32)
    for j in reversed(range(count)):
        out_ref[pl.ds(j * GAIN_ROWS, ROWS), :] = acc
        acc = acc + in_ref[pl.ds(j * GAIN_ROWS, ROWS), :]
        gain = gain + in_ref[pl.ds(j * GAIN_ROWS + ROWS, 1), :]
    for j in range(count):
        out_ref[pl.ds(j * GAIN_ROWS + ROWS, 1), :] = gain


def stats_kernel(q_ref, local_ref, prefix_ref, cot_ref, gain_ref, att_ref, low_ref, out_ref):
    rows, width = q_ref.shape
    squares = jnp.zeros((rows, HEAD_DIM), F32)
    crossed = jnp.zeros((rows, HEAD_DIM), F32)
    for h in range(width // HEAD_DIM):
        low = prefix_ref[pl.ds(h * HEAD_DIM, HEAD_DIM), :].astype(BF16)
        low_ref[pl.ds(h * HEAD_DIM, HEAD_DIM), :] = low
        att = local_ref[:, cols(h)] + dot(q_ref[:, cols(h)], low, 1, 0)
        att_ref[:, cols(h)] = att
        squares = squares + att * att
        crossed = crossed + att * (cot_ref[:, cols(h)].astype(F32) * gain_ref[:, cols(h)])
    parts = rows // HEAD_DIM
    peers = out_ref.shape[0]
    for n, sums in enumerate((squares, crossed)):
        for i in range(parts):
            turned = sums[i * HEAD_DIM : (i + 1) * HEAD_DIM, :].T
            line = jnp.sum(turned, axis=0, keepdims=True)
            for peer in range(peers):
                out_ref[peer, pl.ds(n * parts + i, 1), :] = line


def grads_kernel(att_ref, cot_ref, gain_ref, stats_ref, q_ref, grads_ref, out_ref):
    rows, width = att_ref.shape
    parts = rows // HEAD_DIM
    heads = width // HEAD_DIM
    stats = jnp.sum(stats_ref[...], axis=0)
    inv = lax.rsqrt(stats[:parts] / HD + EPS)
    mean = stats[parts:] * inv / HD
    for i in range(parts):
        mine = pl.ds(i * HEAD_DIM, HEAD_DIM)
        square = (HEAD_DIM, HEAD_DIM)
        inv_i = jnp.broadcast_to(inv[i : i + 1, :], square).T
        mean_i = jnp.broadcast_to(mean[i : i + 1, :], square).T
        for h in range(heads):
            normed = att_ref[mine, cols(h)] * inv_i
            upstream = cot_ref[mine, cols(h)].astype(F32)
            scaled = upstream * gain_ref[:, cols(h)]
            grads_ref[mine, cols(h)] = ((scaled - normed * mean_i) * inv_i).astype(BF16)
            line = jnp.sum(upstream * normed, axis=0, keepdims=True)
            at = pl.ds(h * GAIN_ROWS + ROWS, 1)
            if i == 0:
                out_ref[at, :] = line
            else:
                out_ref[at, :] = out_ref[at, :] + line
    slices = HEAD_DIM // ROWS
    for h in range(heads):
        state = dot(q_ref[:, cols(h)], grads_ref[:, cols(h)], 0, 0)
        for s in range(slices):
            piece = h * slices + s
            out_ref[pl.ds(piece * GAIN_ROWS, ROWS), :] = state[s * ROWS : (s + 1) * ROWS, :]
            if piece >= heads:
                out_ref[pl.ds(piece * GAIN_ROWS + ROWS, 1), :] = jnp.zeros((1, HEAD_DIM), F32)


def backward_kernel(
    q_ref, k_ref, v_ref, grads_ref, weights_ref, low_ref, query_ref, key_ref, value_ref, score_ref
):
    rows = q_ref.shape[0]
    block = min(256, rows)
    for h in range(q_ref.shape[1] // HEAD_DIM):
        low = low_ref[pl.ds(h * HEAD_DIM, HEAD_DIM), :]
        for i in range(rows // block):
            mine = pl.ds(i * block, block)
            ends = (i + 1) * block
            scores = dot(grads_ref[mine, cols(h)], v_ref[:ends, cols(h)], 1, 1)
            score = masked(scores, i * block, 0).astype(BF16)
            score_ref[mine, :ends] = score
            query = dot(score, k_ref[:ends, cols(h)], 1, 0)
            query = query + dot(grads_ref[mine, cols(h)], low, 1, 1)
            query_ref[mine, cols(h)] = query.astype(BF16)
        for i in range(rows // block):
            mine = pl.ds(i * block, block)
            first = i * block
            key_ref[mine, cols(h)] = dot(score_ref[first:, mine], q_ref[first:, cols(h)], 0, 0)
            value_ref[mine, cols(h)] = dot(
                weights_ref[h, first:, mine], grads_ref[first:, cols(h)], 0, 0
            )


def final_kernel(key_ref, value_ref, k_ref, v_ref, suffix_ref, key_out, value_out, gain_out):
    heads = k_ref.shape[1] // HEAD_DIM
    slices = HEAD_DIM // ROWS
    length = suffix_ref.shape[0] // GAIN_ROWS * k_ref.shape[0]
    for h in range(heads):
        pieces = [
            suffix_ref[pl.ds((h * slices + s) * GAIN_ROWS, ROWS), :] for s in range(slices)
        ]
        low = jnp.concatenate(pieces, axis=0).astype(BF16)
        key = key_ref[:, cols(h)] + dot(v_ref[:, cols(h)], low, 1, 1)
        key_out[:, cols(h)] = key.astype(BF16)
        value = value_ref[:, cols(h)] + dot(k_ref[:, cols(h)], low, 1, 0)
        value_out[:, cols(h)] = value.astype(BF16)
        line = suffix_ref[pl.ds(h * GAIN_ROWS + ROWS, 1), :]
        gain_out[pl.ds(h, 1), :] = line * (1.0 / math.sqrt(length))


def exchange(x, axis, shape):
    count = lax.axis_size(axis)
    moved = lax.all_to_all(x.reshape((count,) + shape), axis, 0, 0, tiled=True)
    return moved.reshape(x.shape)


def shards(query, key, value, cotangent, gain):
    rows, width = query.shape
    heads = width // HEAD_DIM
    blocks = lax.axis_size("seq")
    peers = lax.axis_size("fsdp")
    sds = jax.ShapeDtypeStruct
    gain_row = gain.reshape(1, width)
    small = 2 * rows * width * HEAD_DIM
    big = 2 * rows * rows * width

    (state,) = call(state_kernel, [sds((width, HEAD_DIM), F32)], small, key, value)
    slices = exchange(state, "seq", (ROWS, HEAD_DIM))
    weights, local = call(
        local_kernel,
        [sds((heads, rows, rows), BF16), sds((rows, width), F32)],
        2 * big,
        query,
        key,
        value,
    )
    slices = slices.reshape(blocks, ROWS, HEAD_DIM)
    (slices,) = call(prefix_kernel, [sds(slices.shape, F32)], width * HEAD_DIM, slices)
    prefix = exchange(slices.reshape(width, HEAD_DIM), "seq", (ROWS, HEAD_DIM))

    attended, prefix_low, stats = call(
        stats_kernel,
        [
            sds((rows, width), F32),
            sds((width, HEAD_DIM), BF16),
            sds((peers, 2 * rows // HEAD_DIM, HEAD_DIM), F32),
        ],
        small,
        query,
        local,
        prefix,
        cotangent,
        gain_row,
    )
    stats = lax.all_to_all(stats, "fsdp", 0, 0, tiled=True)
    grads, grad_state = call(
        grads_kernel,
        [sds((rows, width), BF16), sds((blocks * GAIN_ROWS, HEAD_DIM), F32)],
        small,
        attended,
        cotangent,
        gain_row,
        stats,
        query,
    )
    grad_slices = exchange(grad_state, "seq", (GAIN_ROWS, 1, HEAD_DIM))
    query_grad, key_local, value_local, _ = call(
        backward_kernel,
        [
            sds((rows, width), BF16),
            sds((rows, width), F32),
            sds((rows, width), F32),
            sds((rows, rows), BF16),
        ],
        4 * big + small,
        query,
        key,
        value,
        grads,
        weights,
        prefix_low,
    )
    (grad_slices,) = call(
        suffix_kernel, [sds(grad_slices.shape, F32)], width * HEAD_DIM, grad_slices
    )
    suffix = exchange(grad_slices, "seq", (GAIN_ROWS, 1, HEAD_DIM))
    key_grad, value_grad, gain_grad = call(
        final_kernel,
        [
            sds((rows, width), BF16),
            sds((rows, width), BF16),
            sds((heads, HEAD_DIM), F32),
        ],
        2 * small,
        key_local,
        value_local,
        key,
        value,
        suffix,
    )
    return query_grad, key_grad, value_grad, gain_grad.reshape(width)


def solution(mesh):
    in_specs = (P("seq", "fsdp"), P("seq", "fsdp"), P("seq", "fsdp"), P("seq", "fsdp"), P("fsdp"))
    out_specs = (P("seq", "fsdp"), P("seq", "fsdp"), P("seq", "fsdp"), P("fsdp"))
    return jax.shard_map(shards, mesh=mesh, in_specs=in_specs, out_specs=out_specs, check_vma=False)
```

```python
import math

import jax
import jax.numpy as jnp
from jax import lax
from jax.experimental import pallas as pl
from jax.experimental.pallas import tpu as pltpu
from jax.sharding import PartitionSpec as P

HEAD_DIM = 128
HD = 4096
EPS = 1e-05
F32 = jnp.float32
BF16 = jnp.bfloat16
VMEM, HBM = pltpu.VMEM, pltpu.HBM
VMEM_LIMIT = 16 * 2**20
ROWS = 8
GAIN_ROWS = ROWS + 1


SEQ_FIRST = 46
FSDP_FIRST = 6


def place_of(j, count):
    return (j - SEQ_FIRST) % count


def groups(first, count):
    return [[(first + i) % count for i in range(count)]]


def dot(a, b, over_a, over_b):
    return lax.dot_general(a, b, (((over_a,), (over_b,)), ((), ())), preferred_element_type=F32)


def cols(h):
    return pl.ds(h * HEAD_DIM, HEAD_DIM)


def call(kernel, outs, flops, *args, scratch=(), homes=None, spaces=None):
    out_bytes = sum(math.prod(o.shape) * jnp.dtype(o.dtype).itemsize for o in outs)
    in_bytes = sum(math.prod(a.shape) * a.dtype.itemsize for a in args)
    return pl.pallas_call(
        kernel,
        out_shape=tuple(outs),
        scratch_shapes=list(scratch),
        in_specs=[pl.BlockSpec(memory_space=s) for s in spaces or [pltpu.VMEM] * len(args)],
        out_specs=tuple(pl.BlockSpec(memory_space=VMEM) for _ in outs),
        cost_estimate=pl.CostEstimate(
            flops=flops, transcendentals=0, bytes_accessed=in_bytes + out_bytes
        ),
        compiler_params=pltpu.CompilerParams(vmem_limit_bytes=VMEM_LIMIT),
        name=kernel.__name__,
    )(*map(pltpu.with_memory_space_constraint, args, homes or [VMEM] * len(args)))


def state_kernel(k_hbm, v_hbm, out_ref, k_ref, v_ref, sems):
    rows, width = k_ref.shape
    heads = width // HEAD_DIM
    parts = sems.shape[1]
    part = rows // parts
    copies = []
    for i in range(parts):
        mine = pl.ds(i * part, part)
        for n, (source, target) in enumerate(((k_hbm, k_ref), (v_hbm, v_ref))):
            copy = pltpu.make_async_copy(source.at[mine], target.at[mine], sems.at[n, i])
            copy.start()
            copies.append(copy)
    states = [jnp.zeros((HEAD_DIM, HEAD_DIM), F32)] * heads
    for i in range(parts):
        copies[2 * i].wait()
        copies[2 * i + 1].wait()
        mine = pl.ds(i * part, part)
        for h in range(heads):
            states[h] = states[h] + dot(k_ref[mine, cols(h)], v_ref[mine, cols(h)], 0, 0)
    for h in range(heads):
        out_ref[pl.ds(h * HEAD_DIM, HEAD_DIM), :] = states[h]


def masked(scores, first_row, first_col):
    row = lax.broadcasted_iota(jnp.int32, scores.shape, 0) + first_row
    col = lax.broadcasted_iota(jnp.int32, scores.shape, 1) + first_col
    return jnp.where(row >= col, scores, 0.0)


def local_kernel(q_ref, k_ref, v_ref, local_ref):
    rows = q_ref.shape[0]
    block = min(256, rows)
    for h in range(q_ref.shape[1] // HEAD_DIM):
        for i in range(rows // block):
            mine = pl.ds(i * block, block)
            ends = (i + 1) * block
            scores = dot(q_ref[mine, cols(h)], k_ref[:ends, cols(h)], 1, 1)
            weights = masked(scores, i * block, 0).astype(BF16)
            local_ref[mine, cols(h)] = dot(weights, v_ref[:ends, cols(h)], 1, 0)


def prefix_kernel(in_ref, out_ref):
    count = in_ref.shape[0]
    acc = jnp.zeros(in_ref.shape[1:], F32)
    for j in range(count):
        at = place_of(j, count)
        out_ref[at] = acc
        acc = acc + in_ref[at]


def suffix_kernel(in_ref, out_ref):
    count = in_ref.shape[0] // GAIN_ROWS
    acc = jnp.zeros((ROWS, HEAD_DIM), F32)
    gain = jnp.zeros((1, HEAD_DIM), F32)
    for j in reversed(range(count)):
        at = place_of(j, count) * GAIN_ROWS
        out_ref[pl.ds(at, ROWS), :] = acc
        acc = acc + in_ref[pl.ds(at, ROWS), :]
        gain = gain + in_ref[pl.ds(at + ROWS, 1), :]
    for j in range(count):
        out_ref[pl.ds(j * GAIN_ROWS + ROWS, 1), :] = gain


def stats_kernel(q_ref, local_ref, prefix_ref, cot_ref, gain_ref, att_ref, out_ref):
    rows, width = q_ref.shape
    squares = jnp.zeros((rows, HEAD_DIM), F32)
    crossed = jnp.zeros((rows, HEAD_DIM), F32)
    for h in range(width // HEAD_DIM):
        low = prefix_ref[pl.ds(h * HEAD_DIM, HEAD_DIM), :].astype(BF16)
        att = local_ref[:, cols(h)] + dot(q_ref[:, cols(h)], low, 1, 0)
        att_ref[:, cols(h)] = att
        squares = squares + att * att
        crossed = crossed + att * (cot_ref[:, cols(h)].astype(F32) * gain_ref[:, cols(h)])
    parts = rows // HEAD_DIM
    peers = out_ref.shape[0]
    for n, sums in enumerate((squares, crossed)):
        for i in range(parts):
            turned = sums[i * HEAD_DIM : (i + 1) * HEAD_DIM, :].T
            line = jnp.sum(turned, axis=0, keepdims=True)
            for peer in range(peers):
                out_ref[peer, pl.ds(n * parts + i, 1), :] = line


def grads_kernel(att_ref, cot_ref, gain_ref, stats_ref, q_ref, grads_ref, out_ref):
    rows, width = att_ref.shape
    parts = rows // HEAD_DIM
    heads = width // HEAD_DIM
    stats = jnp.sum(stats_ref[...], axis=0)
    inv = lax.rsqrt(stats[:parts] / HD + EPS)
    mean = stats[parts:] * inv / HD
    for i in range(parts):
        mine = pl.ds(i * HEAD_DIM, HEAD_DIM)
        square = (HEAD_DIM, HEAD_DIM)
        inv_i = jnp.broadcast_to(inv[i : i + 1, :], square).T
        mean_i = jnp.broadcast_to(mean[i : i + 1, :], square).T
        for h in range(heads):
            normed = att_ref[mine, cols(h)] * inv_i
            upstream = cot_ref[mine, cols(h)].astype(F32)
            scaled = upstream * gain_ref[:, cols(h)]
            grads_ref[mine, cols(h)] = ((scaled - normed * mean_i) * inv_i).astype(BF16)
            line = jnp.sum(upstream * normed, axis=0, keepdims=True)
            at = pl.ds(h * GAIN_ROWS + ROWS, 1)
            if i == 0:
                out_ref[at, :] = line
            else:
                out_ref[at, :] = out_ref[at, :] + line
    slices = HEAD_DIM // ROWS
    for h in range(heads):
        state = dot(q_ref[:, cols(h)], grads_ref[:, cols(h)], 0, 0)
        for s in range(slices):
            piece = h * slices + s
            out_ref[pl.ds(piece * GAIN_ROWS, ROWS), :] = state[s * ROWS : (s + 1) * ROWS, :]
            if piece >= heads:
                out_ref[pl.ds(piece * GAIN_ROWS + ROWS, 1), :] = jnp.zeros((1, HEAD_DIM), F32)


def backward_kernel(
    q_ref, k_ref, v_ref, grads_ref, prefix_ref, query_ref, key_ref, value_ref, weights_ref, score_ref
):
    rows = q_ref.shape[0]
    block = min(256, rows)
    for h in range(q_ref.shape[1] // HEAD_DIM):
        low = prefix_ref[pl.ds(h * HEAD_DIM, HEAD_DIM), :].astype(BF16)
        for i in range(rows // block):
            mine = pl.ds(i * block, block)
            ends = (i + 1) * block
            grads = grads_ref[mine, cols(h)]
            keys = k_ref[:ends, cols(h)]
            scores = dot(q_ref[mine, cols(h)], keys, 1, 1)
            weights_ref[mine, :ends] = masked(scores, i * block, 0).astype(BF16)
            scores = dot(grads, v_ref[:ends, cols(h)], 1, 1)
            score = masked(scores, i * block, 0).astype(BF16)
            score_ref[mine, :ends] = score
            query = dot(score, keys, 1, 0) + dot(grads, low, 1, 1)
            query_ref[mine, cols(h)] = query.astype(BF16)
        for i in range(rows // block):
            mine = pl.ds(i * block, block)
            first = i * block
            key_ref[mine, cols(h)] = dot(score_ref[first:, mine], q_ref[first:, cols(h)], 0, 0)
            value_ref[mine, cols(h)] = dot(
                weights_ref[first:, mine], grads_ref[first:, cols(h)], 0, 0
            )


def final_kernel(key_ref, value_ref, k_ref, v_ref, suffix_ref, key_out, value_out, gain_out):
    rows, width = k_ref.shape
    slices = HEAD_DIM // ROWS
    length = suffix_ref.shape[0] // GAIN_ROWS * rows
    for h in range(width // HEAD_DIM):
        pieces = [
            suffix_ref[pl.ds((h * slices + s) * GAIN_ROWS, ROWS), :] for s in range(slices)
        ]
        low = jnp.concatenate(pieces, axis=0).astype(BF16)
        key = key_ref[:, cols(h)] + dot(v_ref[:, cols(h)], low, 1, 1)
        key_out[:, cols(h)] = key.astype(BF16)
        value = value_ref[:, cols(h)] + dot(k_ref[:, cols(h)], low, 1, 0)
        value_out[:, cols(h)] = value.astype(BF16)
        line = suffix_ref[pl.ds(h * GAIN_ROWS + ROWS, 1), :]
        gain_out[pl.ds(h, 1), :] = line * (1.0 / math.sqrt(length))


def exchange(x, axis, first, shape):
    count = lax.axis_size(axis)
    moved = lax.all_to_all(
        x.reshape((count,) + shape),
        axis,
        0,
        0,
        axis_index_groups=groups(first, count),
        tiled=True,
    )
    return moved.reshape(x.shape)


def shards(query, key, value, cotangent, gain):
    rows, width = query.shape
    heads = width // HEAD_DIM
    blocks = lax.axis_size("seq")
    peers = lax.axis_size("fsdp")
    sds, vmem = jax.ShapeDtypeStruct, pltpu.VMEM
    gain_row = gain.reshape(1, width)
    small = 2 * rows * width * HEAD_DIM
    big = 2 * rows * rows * width

    (state,) = call(
        state_kernel,
        [vmem((width, HEAD_DIM), F32)],
        small,
        key,
        value,
        scratch=[
            VMEM((rows, width), BF16),
            VMEM((rows, width), BF16),
            pltpu.SemaphoreType.DMA((2, 2)),
        ],
        homes=[HBM] * 2,
        spaces=[HBM] * 2,
    )
    slices = exchange(state, "seq", SEQ_FIRST, (ROWS, HEAD_DIM))
    (local,) = call(
        local_kernel,
        [vmem((rows, width), F32)],
        2 * big,
        query,
        key,
        value,
        homes=[HBM] * 3,
    )
    slices = slices.reshape(blocks, ROWS, HEAD_DIM)
    (slices,) = call(prefix_kernel, [vmem(slices.shape, F32)], width * HEAD_DIM, slices)
    prefix = exchange(slices.reshape(width, HEAD_DIM), "seq", SEQ_FIRST, (ROWS, HEAD_DIM))

    attended, stats = call(
        stats_kernel,
        [
            vmem((rows, width), F32),
            vmem((peers, 2 * rows // HEAD_DIM, HEAD_DIM), F32),
        ],
        small,
        query,
        local,
        prefix,
        cotangent,
        gain_row,
    )
    stats = exchange(stats, "fsdp", FSDP_FIRST, stats.shape[1:])
    grads, grad_state = call(
        grads_kernel,
        [vmem((rows, width), BF16), sds((blocks * GAIN_ROWS, HEAD_DIM), F32)],
        small,
        attended,
        cotangent,
        gain_row,
        stats,
        query,
    )
    grad_slices = exchange(grad_state, "seq", SEQ_FIRST, (GAIN_ROWS, 1, HEAD_DIM))
    query_grad, key_local, value_local = call(
        backward_kernel,
        [
            sds((rows, width), BF16),
            vmem((rows, width), F32),
            vmem((rows, width), F32),
        ],
        4 * big + small,
        query,
        key,
        value,
        grads,
        prefix,
        scratch=[VMEM((rows, rows), BF16), VMEM((rows, rows), BF16)],
        homes=[HBM] * 5,
    )
    (grad_slices,) = call(
        suffix_kernel, [vmem(grad_slices.shape, F32)], width * HEAD_DIM, grad_slices
    )
    suffix = exchange(grad_slices, "seq", SEQ_FIRST, (GAIN_ROWS, 1, HEAD_DIM))
    key_grad, value_grad, gain_grad = call(
        final_kernel,
        [
            sds((rows, width), BF16),
            sds((rows, width), BF16),
            sds((heads, HEAD_DIM), F32),
        ],
        2 * small,
        key_local,
        value_local,
        key,
        value,
        suffix,
    )
    return query_grad, key_grad, value_grad, gain_grad.reshape(width)


def solution(mesh):
    in_specs = (P("seq", "fsdp"), P("seq", "fsdp"), P("seq", "fsdp"), P("seq", "fsdp"), P("fsdp"))
    out_specs = (P("seq", "fsdp"), P("seq", "fsdp"), P("seq", "fsdp"), P("fsdp"))
    return jax.shard_map(shards, mesh=mesh, in_specs=in_specs, out_specs=out_specs, check_vma=False)
```

```python
import math

import jax
import jax.numpy as jnp
from jax import lax
from jax.experimental import pallas as pl
from jax.experimental.pallas import tpu as pltpu
from jax.sharding import PartitionSpec as P

HEAD_DIM = 128
HD = 4096
EPS = 1e-05
F32 = jnp.float32
BF16 = jnp.bfloat16
VMEM, HBM = pltpu.VMEM, pltpu.HBM
VMEM_LIMIT = 16 * 2**20
ROWS = 8
GAIN_ROWS = ROWS + 1
SEQ_FIRST = 45
FSDP_FIRST = 4


def place_of(j, count):
    return (j - SEQ_FIRST) % count


def groups(first, count):
    return [[(first + i) % count for i in range(count)]]


def dot(a, b, over_a, over_b):
    return lax.dot_general(a, b, (((over_a,), (over_b,)), ((), ())), preferred_element_type=F32)


def cols(h):
    return pl.ds(h * HEAD_DIM, HEAD_DIM)


def call(kernel, outs, flops, *args, scratch=(), homes=None, spaces=None):
    out_bytes = sum(math.prod(o.shape) * jnp.dtype(o.dtype).itemsize for o in outs)
    in_bytes = sum(math.prod(a.shape) * a.dtype.itemsize for a in args)
    return pl.pallas_call(
        kernel,
        out_shape=tuple(outs),
        scratch_shapes=list(scratch),
        in_specs=[pl.BlockSpec(memory_space=s) for s in spaces or [pltpu.VMEM] * len(args)],
        out_specs=tuple(pl.BlockSpec(memory_space=VMEM) for _ in outs),
        cost_estimate=pl.CostEstimate(
            flops=flops, transcendentals=0, bytes_accessed=in_bytes + out_bytes
        ),
        compiler_params=pltpu.CompilerParams(vmem_limit_bytes=VMEM_LIMIT),
        name=kernel.__name__,
    )(*map(pltpu.with_memory_space_constraint, args, homes or [VMEM] * len(args)))


def state_kernel(k_hbm, v_hbm, out_ref, k_ref, v_ref, sems):
    rows, width = k_ref.shape
    heads = width // HEAD_DIM
    parts = sems.shape[1]
    part = rows // parts
    copies = []
    for i in range(parts):
        mine = pl.ds(i * part, part)
        for n, (source, target) in enumerate(((k_hbm, k_ref), (v_hbm, v_ref))):
            copy = pltpu.make_async_copy(source.at[mine], target.at[mine], sems.at[n, i])
            copy.start()
            copies.append(copy)
    states = [jnp.zeros((HEAD_DIM, HEAD_DIM), F32)] * heads
    for i in range(parts):
        copies[2 * i].wait()
        copies[2 * i + 1].wait()
        mine = pl.ds(i * part, part)
        for h in range(heads):
            states[h] = states[h] + dot(k_ref[mine, cols(h)], v_ref[mine, cols(h)], 0, 0)
    for h in range(heads):
        out_ref[pl.ds(h * HEAD_DIM, HEAD_DIM), :] = states[h]


def masked(scores, first_row, first_col):
    row = lax.broadcasted_iota(jnp.int32, scores.shape, 0) + first_row
    col = lax.broadcasted_iota(jnp.int32, scores.shape, 1) + first_col
    return jnp.where(row >= col, scores, 0.0)


def local_kernel(q_ref, k_ref, v_ref, local_ref):
    rows = q_ref.shape[0]
    block = min(256, rows)
    for h in range(q_ref.shape[1] // HEAD_DIM):
        for i in range(rows // block):
            mine = pl.ds(i * block, block)
            ends = (i + 1) * block
            scores = dot(q_ref[mine, cols(h)], k_ref[:ends, cols(h)], 1, 1)
            weights = masked(scores, i * block, 0).astype(BF16)
            local_ref[mine, cols(h)] = dot(weights, v_ref[:ends, cols(h)], 1, 0)


def prefix_kernel(in_ref, out_ref):
    count = in_ref.shape[0]
    acc = jnp.zeros(in_ref.shape[1:], F32)
    for j in range(count):
        at = place_of(j, count)
        out_ref[at] = acc
        acc = acc + in_ref[at]


def suffix_kernel(in_ref, out_ref):
    count = in_ref.shape[0] // GAIN_ROWS
    acc = jnp.zeros((ROWS, HEAD_DIM), F32)
    gain = jnp.zeros((1, HEAD_DIM), F32)
    for j in reversed(range(count)):
        at = place_of(j, count) * GAIN_ROWS
        out_ref[pl.ds(at, ROWS), :] = acc
        acc = acc + in_ref[pl.ds(at, ROWS), :]
        gain = gain + in_ref[pl.ds(at + ROWS, 1), :]
    for j in range(count):
        out_ref[pl.ds(j * GAIN_ROWS + ROWS, 1), :] = gain


def stats_kernel(q_ref, local_ref, prefix_ref, cot_ref, gain_ref, att_ref, out_ref):
    rows, width = q_ref.shape
    squares = jnp.zeros((rows, HEAD_DIM), F32)
    crossed = jnp.zeros((rows, HEAD_DIM), F32)
    for h in range(width // HEAD_DIM):
        low = prefix_ref[pl.ds(h * HEAD_DIM, HEAD_DIM), :].astype(BF16)
        att = local_ref[:, cols(h)] + dot(q_ref[:, cols(h)], low, 1, 0)
        att_ref[:, cols(h)] = att
        squares = squares + att * att
        crossed = crossed + att * (cot_ref[:, cols(h)].astype(F32) * gain_ref[:, cols(h)])
    parts = rows // HEAD_DIM
    peers = out_ref.shape[0]
    for n, sums in enumerate((squares, crossed)):
        for i in range(parts):
            turned = sums[i * HEAD_DIM : (i + 1) * HEAD_DIM, :].T
            line = jnp.sum(turned, axis=0, keepdims=True)
            for peer in range(peers):
                out_ref[peer, pl.ds(n * parts + i, 1), :] = line


def grads_kernel(att_ref, cot_ref, gain_ref, stats_ref, q_ref, grads_ref, out_ref):
    rows, width = att_ref.shape
    parts = rows // HEAD_DIM
    heads = width // HEAD_DIM
    stats = jnp.sum(stats_ref[...], axis=0)
    inv = lax.rsqrt(stats[:parts] / HD + EPS)
    mean = stats[parts:] * inv / HD
    for i in range(parts):
        mine = pl.ds(i * HEAD_DIM, HEAD_DIM)
        square = (HEAD_DIM, HEAD_DIM)
        inv_i = jnp.broadcast_to(inv[i : i + 1, :], square).T
        mean_i = jnp.broadcast_to(mean[i : i + 1, :], square).T
        for h in range(heads):
            normed = att_ref[mine, cols(h)] * inv_i
            upstream = cot_ref[mine, cols(h)].astype(F32)
            scaled = upstream * gain_ref[:, cols(h)]
            grads_ref[mine, cols(h)] = ((scaled - normed * mean_i) * inv_i).astype(BF16)
            line = jnp.sum(upstream * normed, axis=0, keepdims=True)
            at = pl.ds(h * GAIN_ROWS + ROWS, 1)
            if i == 0:
                out_ref[at, :] = line
            else:
                out_ref[at, :] = out_ref[at, :] + line
    slices = HEAD_DIM // ROWS
    for h in range(heads):
        state = dot(q_ref[:, cols(h)], grads_ref[:, cols(h)], 0, 0)
        for s in range(slices):
            piece = h * slices + s
            out_ref[pl.ds(piece * GAIN_ROWS, ROWS), :] = state[s * ROWS : (s + 1) * ROWS, :]
            if piece >= heads:
                out_ref[pl.ds(piece * GAIN_ROWS + ROWS, 1), :] = jnp.zeros((1, HEAD_DIM), F32)


def backward_kernel(
    q_ref, k_ref, v_ref, grads_ref, prefix_ref, query_ref, key_ref, value_ref, weights_ref, score_ref
):
    rows = q_ref.shape[0]
    block = min(256, rows)
    for h in range(q_ref.shape[1] // HEAD_DIM):
        low = prefix_ref[pl.ds(h * HEAD_DIM, HEAD_DIM), :].astype(BF16)
        for i in range(rows // block):
            mine = pl.ds(i * block, block)
            ends = (i + 1) * block
            grads = grads_ref[mine, cols(h)]
            keys = k_ref[:ends, cols(h)]
            scores = dot(q_ref[mine, cols(h)], keys, 1, 1)
            weights_ref[mine, :ends] = masked(scores, i * block, 0).astype(BF16)
            scores = dot(grads, v_ref[:ends, cols(h)], 1, 1)
            score = masked(scores, i * block, 0).astype(BF16)
            score_ref[mine, :ends] = score
            query = dot(score, keys, 1, 0) + dot(grads, low, 1, 1)
            query_ref[mine, cols(h)] = query.astype(BF16)
        for i in range(rows // block):
            mine = pl.ds(i * block, block)
            first = i * block
            key_ref[mine, cols(h)] = dot(score_ref[first:, mine], q_ref[first:, cols(h)], 0, 0)
            value_ref[mine, cols(h)] = dot(
                weights_ref[first:, mine], grads_ref[first:, cols(h)], 0, 0
            )


def final_kernel(key_ref, value_ref, k_ref, v_ref, suffix_ref, key_out, value_out, gain_out):
    rows, width = k_ref.shape
    slices = HEAD_DIM // ROWS
    length = suffix_ref.shape[0] // GAIN_ROWS * rows
    for h in range(width // HEAD_DIM):
        pieces = [
            suffix_ref[pl.ds((h * slices + s) * GAIN_ROWS, ROWS), :] for s in range(slices)
        ]
        low = jnp.concatenate(pieces, axis=0).astype(BF16)
        key = key_ref[:, cols(h)] + dot(v_ref[:, cols(h)], low, 1, 1)
        key_out[:, cols(h)] = key.astype(BF16)
        value = value_ref[:, cols(h)] + dot(k_ref[:, cols(h)], low, 1, 0)
        value_out[:, cols(h)] = value.astype(BF16)
        line = suffix_ref[pl.ds(h * GAIN_ROWS + ROWS, 1), :]
        gain_out[pl.ds(h, 1), :] = line * (1.0 / math.sqrt(length))


def exchange(x, axis, first, shape):
    count = lax.axis_size(axis)
    moved = lax.all_to_all(
        x.reshape((count,) + shape),
        axis,
        0,
        0,
        axis_index_groups=groups(first, count),
        tiled=True,
    )
    return moved.reshape(x.shape)


def shards(query, key, value, cotangent, gain):
    rows, width = query.shape
    heads = width // HEAD_DIM
    blocks = lax.axis_size("seq")
    peers = lax.axis_size("fsdp")
    sds, vmem = jax.ShapeDtypeStruct, pltpu.VMEM
    gain_row = gain.reshape(1, width)
    small = 2 * rows * width * HEAD_DIM
    big = 2 * rows * rows * width

    (state,) = call(
        state_kernel,
        [vmem((width, HEAD_DIM), F32)],
        small,
        key,
        value,
        scratch=[
            VMEM((rows, width), BF16),
            VMEM((rows, width), BF16),
            pltpu.SemaphoreType.DMA((2, 2)),
        ],
        homes=[HBM] * 2,
        spaces=[HBM] * 2,
    )
    slices = exchange(state, "seq", SEQ_FIRST, (ROWS, HEAD_DIM))
    (local,) = call(
        local_kernel,
        [vmem((rows, width), F32)],
        2 * big,
        query,
        key,
        value,
        homes=[HBM] * 3,
    )
    slices = slices.reshape(blocks, ROWS, HEAD_DIM)
    (slices,) = call(prefix_kernel, [vmem(slices.shape, F32)], width * HEAD_DIM, slices)
    prefix = exchange(slices.reshape(width, HEAD_DIM), "seq", SEQ_FIRST, (ROWS, HEAD_DIM))

    attended, stats = call(
        stats_kernel,
        [
            vmem((rows, width), F32),
            vmem((peers, 2 * rows // HEAD_DIM, HEAD_DIM), F32),
        ],
        small,
        query,
        local,
        prefix,
        cotangent,
        gain_row,
    )
    stats = exchange(stats, "fsdp", FSDP_FIRST, stats.shape[1:])
    grads, grad_state = call(
        grads_kernel,
        [vmem((rows, width), BF16), sds((blocks * GAIN_ROWS, HEAD_DIM), F32)],
        small,
        attended,
        cotangent,
        gain_row,
        stats,
        query,
    )
    grad_slices = exchange(grad_state, "seq", SEQ_FIRST, (GAIN_ROWS, 1, HEAD_DIM))
    query_grad, key_local, value_local = call(
        backward_kernel,
        [
            sds((rows, width), BF16),
            vmem((rows, width), F32),
            vmem((rows, width), F32),
        ],
        4 * big + small,
        query,
        key,
        value,
        grads,
        prefix,
        scratch=[VMEM((rows, rows), BF16), VMEM((rows, rows), BF16)],
        homes=[HBM] * 5,
    )
    (grad_slices,) = call(
        suffix_kernel, [vmem(grad_slices.shape, F32)], width * HEAD_DIM, grad_slices
    )
    suffix = exchange(grad_slices, "seq", SEQ_FIRST, (GAIN_ROWS, 1, HEAD_DIM))
    key_grad, value_grad, gain_grad = call(
        final_kernel,
        [
            sds((rows, width), BF16),
            sds((rows, width), BF16),
            sds((heads, HEAD_DIM), F32),
        ],
        2 * small,
        key_local,
        value_local,
        key,
        value,
        suffix,
    )
    return query_grad, key_grad, value_grad, gain_grad.reshape(width)


def solution(mesh):
    in_specs = (P("seq", "fsdp"), P("seq", "fsdp"), P("seq", "fsdp"), P("seq", "fsdp"), P("fsdp"))
    out_specs = (P("seq", "fsdp"), P("seq", "fsdp"), P("seq", "fsdp"), P("fsdp"))
    return jax.shard_map(shards, mesh=mesh, in_specs=in_specs, out_specs=out_specs, check_vma=False)
```

```python
import math

import jax
import jax.numpy as jnp
from jax import lax
from jax.experimental import pallas as pl
from jax.experimental.pallas import tpu as pltpu
from jax.sharding import PartitionSpec as P

HEAD_DIM = 128
HD = 4096
EPS = 1e-05
F32 = jnp.float32
BF16 = jnp.bfloat16
VMEM, HBM = pltpu.VMEM, pltpu.HBM
VMEM_LIMIT = 16 * 2**20
ROWS = 8
GAIN_ROWS = ROWS + 1
SEQ_FIRST = 37
FSDP_FIRST = 5


def place_of(j, count):
    return (j - SEQ_FIRST) % count


def groups(first, count):
    return [[(first + i) % count for i in range(count)]]


def dot(a, b, over_a, over_b):
    return lax.dot_general(a, b, (((over_a,), (over_b,)), ((), ())), preferred_element_type=F32)


def cols(h):
    return pl.ds(h * HEAD_DIM, HEAD_DIM)


def call(kernel, outs, flops, *args, scratch=(), homes=None, spaces=None):
    out_bytes = sum(math.prod(o.shape) * jnp.dtype(o.dtype).itemsize for o in outs)
    in_bytes = sum(math.prod(a.shape) * a.dtype.itemsize for a in args)
    return pl.pallas_call(
        kernel,
        out_shape=tuple(outs),
        scratch_shapes=list(scratch),
        in_specs=[pl.BlockSpec(memory_space=s) for s in spaces or [pltpu.VMEM] * len(args)],
        out_specs=tuple(pl.BlockSpec(memory_space=VMEM) for _ in outs),
        cost_estimate=pl.CostEstimate(
            flops=flops, transcendentals=0, bytes_accessed=in_bytes + out_bytes
        ),
        compiler_params=pltpu.CompilerParams(vmem_limit_bytes=VMEM_LIMIT),
        name=kernel.__name__,
    )(*map(pltpu.with_memory_space_constraint, args, homes or [VMEM] * len(args)))


def state_kernel(k_hbm, v_hbm, out_ref, k_ref, v_ref, sems):
    rows, width = k_ref.shape
    heads = width // HEAD_DIM
    parts = sems.shape[1]
    part = rows // parts
    copies = []
    for i in range(parts):
        mine = pl.ds(i * part, part)
        for n, (source, target) in enumerate(((k_hbm, k_ref), (v_hbm, v_ref))):
            copy = pltpu.make_async_copy(source.at[mine], target.at[mine], sems.at[n, i])
            copy.start()
            copies.append(copy)
    states = [jnp.zeros((HEAD_DIM, HEAD_DIM), F32)] * heads
    for i in range(parts):
        copies[2 * i].wait()
        copies[2 * i + 1].wait()
        mine = pl.ds(i * part, part)
        for h in range(heads):
            states[h] = states[h] + dot(k_ref[mine, cols(h)], v_ref[mine, cols(h)], 0, 0)
    for h in range(heads):
        out_ref[pl.ds(h * HEAD_DIM, HEAD_DIM), :] = states[h]


def masked(scores, first_row, first_col):
    row = lax.broadcasted_iota(jnp.int32, scores.shape, 0) + first_row
    col = lax.broadcasted_iota(jnp.int32, scores.shape, 1) + first_col
    return jnp.where(row >= col, scores, 0.0)


def local_kernel(q_ref, k_ref, v_ref, local_ref):
    rows = q_ref.shape[0]
    block = min(256, rows)
    for h in range(q_ref.shape[1] // HEAD_DIM):
        for i in range(rows // block):
            mine = pl.ds(i * block, block)
            ends = (i + 1) * block
            scores = dot(q_ref[mine, cols(h)], k_ref[:ends, cols(h)], 1, 1)
            weights = masked(scores, i * block, 0).astype(BF16)
            local_ref[mine, cols(h)] = dot(weights, v_ref[:ends, cols(h)], 1, 0)


def prefix_kernel(in_ref, out_ref):
    count = in_ref.shape[0]
    acc = jnp.zeros(in_ref.shape[1:], F32)
    for j in range(count):
        at = place_of(j, count)
        out_ref[at] = acc
        acc = acc + in_ref[at]


def suffix_kernel(in_ref, out_ref):
    count = in_ref.shape[0] // GAIN_ROWS
    acc = jnp.zeros((ROWS, HEAD_DIM), F32)
    gain = jnp.zeros((1, HEAD_DIM), F32)
    for j in reversed(range(count)):
        at = place_of(j, count) * GAIN_ROWS
        out_ref[pl.ds(at, ROWS), :] = acc
        acc = acc + in_ref[pl.ds(at, ROWS), :]
        gain = gain + in_ref[pl.ds(at + ROWS, 1), :]
    for j in range(count):
        out_ref[pl.ds(j * GAIN_ROWS + ROWS, 1), :] = gain


def stats_kernel(q_ref, local_ref, prefix_ref, cot_ref, gain_ref, att_ref, out_ref):
    rows, width = q_ref.shape
    squares = jnp.zeros((rows, HEAD_DIM), F32)
    crossed = jnp.zeros((rows, HEAD_DIM), F32)
    for h in range(width // HEAD_DIM):
        low = prefix_ref[pl.ds(h * HEAD_DIM, HEAD_DIM), :].astype(BF16)
        att = local_ref[:, cols(h)] + dot(q_ref[:, cols(h)], low, 1, 0)
        att_ref[:, cols(h)] = att
        squares = squares + att * att
        crossed = crossed + att * (cot_ref[:, cols(h)].astype(F32) * gain_ref[:, cols(h)])
    parts = rows // HEAD_DIM
    peers = out_ref.shape[0]
    for n, sums in enumerate((squares, crossed)):
        for i in range(parts):
            turned = sums[i * HEAD_DIM : (i + 1) * HEAD_DIM, :].T
            line = jnp.sum(turned, axis=0, keepdims=True)
            for peer in range(peers):
                out_ref[peer, pl.ds(n * parts + i, 1), :] = line


def grads_kernel(att_ref, cot_ref, gain_ref, stats_ref, q_ref, grads_ref, out_ref):
    rows, width = att_ref.shape
    parts = rows // HEAD_DIM
    heads = width // HEAD_DIM
    stats = jnp.sum(stats_ref[...], axis=0)
    inv = lax.rsqrt(stats[:parts] / HD + EPS)
    mean = stats[parts:] * inv / HD
    for i in range(parts):
        mine = pl.ds(i * HEAD_DIM, HEAD_DIM)
        square = (HEAD_DIM, HEAD_DIM)
        inv_i = jnp.broadcast_to(inv[i : i + 1, :], square).T
        mean_i = jnp.broadcast_to(mean[i : i + 1, :], square).T
        for h in range(heads):
            normed = att_ref[mine, cols(h)] * inv_i
            upstream = cot_ref[mine, cols(h)].astype(F32)
            scaled = upstream * gain_ref[:, cols(h)]
            grads_ref[mine, cols(h)] = ((scaled - normed * mean_i) * inv_i).astype(BF16)
            line = jnp.sum(upstream * normed, axis=0, keepdims=True)
            at = pl.ds(h * GAIN_ROWS + ROWS, 1)
            if i == 0:
                out_ref[at, :] = line
            else:
                out_ref[at, :] = out_ref[at, :] + line
    slices = HEAD_DIM // ROWS
    for h in range(heads):
        state = dot(q_ref[:, cols(h)], grads_ref[:, cols(h)], 0, 0)
        for s in range(slices):
            piece = h * slices + s
            out_ref[pl.ds(piece * GAIN_ROWS, ROWS), :] = state[s * ROWS : (s + 1) * ROWS, :]
            if piece >= heads:
                out_ref[pl.ds(piece * GAIN_ROWS + ROWS, 1), :] = jnp.zeros((1, HEAD_DIM), F32)


def backward_kernel(
    q_ref, k_ref, v_ref, grads_ref, prefix_ref, query_ref, key_ref, value_ref, weights_ref, score_ref
):
    rows = q_ref.shape[0]
    block = min(256, rows)
    for h in range(q_ref.shape[1] // HEAD_DIM):
        low = prefix_ref[pl.ds(h * HEAD_DIM, HEAD_DIM), :].astype(BF16)
        for i in range(rows // block):
            mine = pl.ds(i * block, block)
            ends = (i + 1) * block
            grads = grads_ref[mine, cols(h)]
            keys = k_ref[:ends, cols(h)]
            scores = dot(q_ref[mine, cols(h)], keys, 1, 1)
            weights_ref[mine, :ends] = masked(scores, i * block, 0).astype(BF16)
            scores = dot(grads, v_ref[:ends, cols(h)], 1, 1)
            score = masked(scores, i * block, 0).astype(BF16)
            score_ref[mine, :ends] = score
            query = dot(score, keys, 1, 0) + dot(grads, low, 1, 1)
            query_ref[mine, cols(h)] = query.astype(BF16)
        for i in range(rows // block):
            mine = pl.ds(i * block, block)
            first = i * block
            key_ref[mine, cols(h)] = dot(score_ref[first:, mine], q_ref[first:, cols(h)], 0, 0)
            value_ref[mine, cols(h)] = dot(
                weights_ref[first:, mine], grads_ref[first:, cols(h)], 0, 0
            )


def final_kernel(key_ref, value_ref, k_ref, v_ref, suffix_ref, key_out, value_out, gain_out):
    rows, width = k_ref.shape
    slices = HEAD_DIM // ROWS
    length = suffix_ref.shape[0] // GAIN_ROWS * rows
    for h in range(width // HEAD_DIM):
        pieces = [
            suffix_ref[pl.ds((h * slices + s) * GAIN_ROWS, ROWS), :] for s in range(slices)
        ]
        low = jnp.concatenate(pieces, axis=0).astype(BF16)
        key = key_ref[:, cols(h)] + dot(v_ref[:, cols(h)], low, 1, 1)
        key_out[:, cols(h)] = key.astype(BF16)
        value = value_ref[:, cols(h)] + dot(k_ref[:, cols(h)], low, 1, 0)
        value_out[:, cols(h)] = value.astype(BF16)
        line = suffix_ref[pl.ds(h * GAIN_ROWS + ROWS, 1), :]
        gain_out[pl.ds(h, 1), :] = line * (1.0 / math.sqrt(length))


def exchange(x, axis, first, shape):
    count = lax.axis_size(axis)
    moved = lax.all_to_all(
        x.reshape((count,) + shape),
        axis,
        0,
        0,
        axis_index_groups=groups(first, count),
        tiled=True,
    )
    return moved.reshape(x.shape)


def shards(query, key, value, cotangent, gain):
    rows, width = query.shape
    heads = width // HEAD_DIM
    blocks = lax.axis_size("seq")
    peers = lax.axis_size("fsdp")
    sds, vmem = jax.ShapeDtypeStruct, pltpu.VMEM
    gain_row = gain.reshape(1, width)
    small = 2 * rows * width * HEAD_DIM
    big = 2 * rows * rows * width

    (state,) = call(
        state_kernel,
        [vmem((width, HEAD_DIM), F32)],
        small,
        key,
        value,
        scratch=[
            VMEM((rows, width), BF16),
            VMEM((rows, width), BF16),
            pltpu.SemaphoreType.DMA((2, 2)),
        ],
        homes=[HBM] * 2,
        spaces=[HBM] * 2,
    )
    slices = exchange(state, "seq", SEQ_FIRST, (ROWS, HEAD_DIM))
    (local,) = call(
        local_kernel,
        [vmem((rows, width), F32)],
        2 * big,
        query,
        key,
        value,
        homes=[HBM] * 3,
    )
    slices = slices.reshape(blocks, ROWS, HEAD_DIM)
    (slices,) = call(prefix_kernel, [vmem(slices.shape, F32)], width * HEAD_DIM, slices)
    prefix = exchange(slices.reshape(width, HEAD_DIM), "seq", SEQ_FIRST, (ROWS, HEAD_DIM))

    attended, stats = call(
        stats_kernel,
        [
            vmem((rows, width), F32),
            vmem((peers, 2 * rows // HEAD_DIM, HEAD_DIM), F32),
        ],
        small,
        query,
        local,
        prefix,
        cotangent,
        gain_row,
    )
    stats = exchange(stats, "fsdp", FSDP_FIRST, stats.shape[1:])
    grads, grad_state = call(
        grads_kernel,
        [vmem((rows, width), BF16), sds((blocks * GAIN_ROWS, HEAD_DIM), F32)],
        small,
        attended,
        cotangent,
        gain_row,
        stats,
        query,
    )
    grad_slices = exchange(grad_state, "seq", SEQ_FIRST, (GAIN_ROWS, 1, HEAD_DIM))
    query_grad, key_local, value_local = call(
        backward_kernel,
        [
            sds((rows, width), BF16),
            vmem((rows, width), F32),
            vmem((rows, width), F32),
        ],
        4 * big + small,
        query,
        key,
        value,
        grads,
        prefix,
        scratch=[VMEM((rows, rows), BF16), VMEM((rows, rows), BF16)],
        homes=[HBM] * 5,
    )
    (grad_slices,) = call(
        suffix_kernel, [vmem(grad_slices.shape, F32)], width * HEAD_DIM, grad_slices
    )
    suffix = exchange(grad_slices, "seq", SEQ_FIRST, (GAIN_ROWS, 1, HEAD_DIM))
    key_grad, value_grad, gain_grad = call(
        final_kernel,
        [
            sds((rows, width), BF16),
            sds((rows, width), BF16),
            sds((heads, HEAD_DIM), F32),
        ],
        2 * small,
        key_local,
        value_local,
        key,
        value,
        suffix,
    )
    return query_grad, key_grad, value_grad, gain_grad.reshape(width)


def solution(mesh):
    in_specs = (P("seq", "fsdp"), P("seq", "fsdp"), P("seq", "fsdp"), P("seq", "fsdp"), P("fsdp"))
    out_specs = (P("seq", "fsdp"), P("seq", "fsdp"), P("seq", "fsdp"), P("fsdp"))
    return jax.shard_map(shards, mesh=mesh, in_specs=in_specs, out_specs=out_specs, check_vma=False)
```

```python
import math

import jax
import jax.numpy as jnp
from jax import lax
from jax.experimental import pallas as pl
from jax.experimental.pallas import tpu as pltpu
from jax.sharding import PartitionSpec as P

HEAD_DIM = 128
HD = 4096
EPS = 1e-05
F32 = jnp.float32
BF16 = jnp.bfloat16
VMEM, HBM = pltpu.VMEM, pltpu.HBM
VMEM_LIMIT = 16 * 2**20
ROWS = 8
GAIN_ROWS = ROWS + 1
SEQ_FIRST = 37
FSDP_FIRST = 5


def place_of(j, count):
    return (j - SEQ_FIRST) % count


def groups(first, count):
    return [[(first + i) % count for i in range(count)]]


def dot(a, b, over_a, over_b):
    return lax.dot_general(a, b, (((over_a,), (over_b,)), ((), ())), preferred_element_type=F32)


def cols(h):
    return pl.ds(h * HEAD_DIM, HEAD_DIM)


def call(kernel, outs, flops, *args, scratch=(), homes=None, spaces=None):
    out_bytes = sum(math.prod(o.shape) * jnp.dtype(o.dtype).itemsize for o in outs)
    in_bytes = sum(math.prod(a.shape) * a.dtype.itemsize for a in args)
    return pl.pallas_call(
        kernel,
        out_shape=tuple(outs),
        scratch_shapes=list(scratch),
        in_specs=[pl.BlockSpec(memory_space=s) for s in spaces or [pltpu.VMEM] * len(args)],
        out_specs=tuple(pl.BlockSpec(memory_space=VMEM) for _ in outs),
        cost_estimate=pl.CostEstimate(
            flops=flops, transcendentals=0, bytes_accessed=in_bytes + out_bytes
        ),
        compiler_params=pltpu.CompilerParams(vmem_limit_bytes=VMEM_LIMIT),
        name=kernel.__name__,
    )(*map(pltpu.with_memory_space_constraint, args, homes or [VMEM] * len(args)))


def state_kernel(k_hbm, v_hbm, out_ref, k_ref, v_ref, sems):
    rows, width = k_ref.shape
    heads = width // HEAD_DIM
    parts = sems.shape[1]
    part = rows // parts
    copies = []
    for i in range(parts):
        mine = pl.ds(i * part, part)
        for n, (source, target) in enumerate(((k_hbm, k_ref), (v_hbm, v_ref))):
            copy = pltpu.make_async_copy(source.at[mine], target.at[mine], sems.at[n, i])
            copy.start()
            copies.append(copy)
    states = [jnp.zeros((HEAD_DIM, HEAD_DIM), F32)] * heads
    for i in range(parts):
        copies[2 * i].wait()
        copies[2 * i + 1].wait()
        mine = pl.ds(i * part, part)
        for h in range(heads):
            states[h] = states[h] + dot(k_ref[mine, cols(h)], v_ref[mine, cols(h)], 0, 0)
    for h in range(heads):
        out_ref[pl.ds(h * HEAD_DIM, HEAD_DIM), :] = states[h]


def masked(scores, first_row, first_col):
    row = lax.broadcasted_iota(jnp.int32, scores.shape, 0) + first_row
    col = lax.broadcasted_iota(jnp.int32, scores.shape, 1) + first_col
    return jnp.where(row >= col, scores, 0.0)


def local_kernel(q_ref, k_ref, v_ref, local_ref):
    rows = q_ref.shape[0]
    block = min(256, rows)
    for h in range(q_ref.shape[1] // HEAD_DIM):
        for i in range(rows // block):
            mine = pl.ds(i * block, block)
            ends = (i + 1) * block
            scores = dot(q_ref[mine, cols(h)], k_ref[:ends, cols(h)], 1, 1)
            weights = masked(scores, i * block, 0).astype(BF16)
            local_ref[mine, cols(h)] = dot(weights, v_ref[:ends, cols(h)], 1, 0)


def prefix_kernel(in_ref, out_ref):
    count = in_ref.shape[0]
    acc = jnp.zeros(in_ref.shape[1:], F32)
    for j in range(count):
        at = place_of(j, count)
        out_ref[at] = acc
        acc = acc + in_ref[at]


def suffix_kernel(in_ref, out_ref):
    count = in_ref.shape[0] // GAIN_ROWS
    acc = jnp.zeros((ROWS, HEAD_DIM), F32)
    gain = jnp.zeros((1, HEAD_DIM), F32)
    for j in reversed(range(count)):
        at = place_of(j, count) * GAIN_ROWS
        out_ref[pl.ds(at, ROWS), :] = acc
        acc = acc + in_ref[pl.ds(at, ROWS), :]
        gain = gain + in_ref[pl.ds(at + ROWS, 1), :]
    for j in range(count):
        out_ref[pl.ds(j * GAIN_ROWS + ROWS, 1), :] = gain


def stats_kernel(q_ref, local_ref, prefix_ref, cot_ref, gain_ref, att_ref, out_ref):
    rows, width = q_ref.shape
    squares = jnp.zeros((rows, HEAD_DIM), F32)
    crossed = jnp.zeros((rows, HEAD_DIM), F32)
    for h in range(width // HEAD_DIM):
        low = prefix_ref[pl.ds(h * HEAD_DIM, HEAD_DIM), :].astype(BF16)
        att = local_ref[:, cols(h)] + dot(q_ref[:, cols(h)], low, 1, 0)
        att_ref[:, cols(h)] = att
        squares = squares + att * att
        crossed = crossed + att * (cot_ref[:, cols(h)].astype(F32) * gain_ref[:, cols(h)])
    parts = rows // HEAD_DIM
    peers = out_ref.shape[0]
    for n, sums in enumerate((squares, crossed)):
        for i in range(parts):
            turned = sums[i * HEAD_DIM : (i + 1) * HEAD_DIM, :].T
            line = jnp.sum(turned, axis=0, keepdims=True)
            for peer in range(peers):
                out_ref[peer, pl.ds(n * parts + i, 1), :] = line


def grads_kernel(att_ref, cot_ref, gain_ref, stats_ref, q_ref, grads_ref, out_ref):
    rows, width = att_ref.shape
    parts = rows // HEAD_DIM
    heads = width // HEAD_DIM
    stats = jnp.sum(stats_ref[...], axis=0)
    inv = lax.rsqrt(stats[:parts] / HD + EPS)
    mean = stats[parts:] * inv / HD
    for i in range(parts):
        mine = pl.ds(i * HEAD_DIM, HEAD_DIM)
        square = (HEAD_DIM, HEAD_DIM)
        inv_i = jnp.broadcast_to(inv[i : i + 1, :], square).T
        mean_i = jnp.broadcast_to(mean[i : i + 1, :], square).T
        for h in range(heads):
            normed = att_ref[mine, cols(h)] * inv_i
            upstream = cot_ref[mine, cols(h)].astype(F32)
            scaled = upstream * gain_ref[:, cols(h)]
            grads_ref[mine, cols(h)] = ((scaled - normed * mean_i) * inv_i).astype(BF16)
            line = jnp.sum(upstream * normed, axis=0, keepdims=True)
            at = pl.ds(h * GAIN_ROWS + ROWS, 1)
            if i == 0:
                out_ref[at, :] = line
            else:
                out_ref[at, :] = out_ref[at, :] + line
    slices = HEAD_DIM // ROWS
    for h in range(heads):
        state = dot(q_ref[:, cols(h)], grads_ref[:, cols(h)], 0, 0)
        for s in range(slices):
            piece = h * slices + s
            out_ref[pl.ds(piece * GAIN_ROWS, ROWS), :] = state[s * ROWS : (s + 1) * ROWS, :]
            if piece >= heads:
                out_ref[pl.ds(piece * GAIN_ROWS + ROWS, 1), :] = jnp.zeros((1, HEAD_DIM), F32)


def backward_kernel(
    q_ref, k_ref, v_ref, grads_ref, prefix_ref, query_ref, key_ref, value_ref, weights_ref, score_ref
):
    rows = q_ref.shape[0]
    block = min(256, rows)
    for h in range(q_ref.shape[1] // HEAD_DIM):
        low = prefix_ref[pl.ds(h * HEAD_DIM, HEAD_DIM), :].astype(BF16)
        for i in range(rows // block):
            mine = pl.ds(i * block, block)
            ends = (i + 1) * block
            grads = grads_ref[mine, cols(h)]
            keys = k_ref[:ends, cols(h)]
            scores = dot(q_ref[mine, cols(h)], keys, 1, 1)
            weights_ref[mine, :ends] = masked(scores, i * block, 0).astype(BF16)
            scores = dot(grads, v_ref[:ends, cols(h)], 1, 1)
            score = masked(scores, i * block, 0).astype(BF16)
            score_ref[mine, :ends] = score
            query = dot(score, keys, 1, 0) + dot(grads, low, 1, 1)
            query_ref[mine, cols(h)] = query.astype(BF16)
        for i in range(rows // block):
            mine = pl.ds(i * block, block)
            first = i * block
            key_ref[mine, cols(h)] = dot(score_ref[first:, mine], q_ref[first:, cols(h)], 0, 0)
            value_ref[mine, cols(h)] = dot(
                weights_ref[first:, mine], grads_ref[first:, cols(h)], 0, 0
            )


def final_kernel(key_ref, value_ref, k_ref, v_ref, suffix_ref, key_out, value_out, gain_out):
    rows, width = k_ref.shape
    slices = HEAD_DIM // ROWS
    length = suffix_ref.shape[0] // GAIN_ROWS * rows
    for h in range(width // HEAD_DIM):
        pieces = [
            suffix_ref[pl.ds((h * slices + s) * GAIN_ROWS, ROWS), :] for s in range(slices)
        ]
        low = jnp.concatenate(pieces, axis=0).astype(BF16)
        key = key_ref[:, cols(h)] + dot(v_ref[:, cols(h)], low, 1, 1)
        key_out[:, cols(h)] = key.astype(BF16)
        value = value_ref[:, cols(h)] + dot(k_ref[:, cols(h)], low, 1, 0)
        value_out[:, cols(h)] = value.astype(BF16)
        line = suffix_ref[pl.ds(h * GAIN_ROWS + ROWS, 1), :]
        gain_out[pl.ds(h, 1), :] = line * (1.0 / math.sqrt(length))


def exchange(x, axis, first, shape):
    count = lax.axis_size(axis)
    moved = lax.all_to_all(
        x.reshape((count,) + shape),
        axis,
        0,
        0,
        axis_index_groups=groups(first, count),
        tiled=True,
    )
    return moved.reshape(x.shape)


def shards(query, key, value, cotangent, gain):
    rows, width = query.shape
    heads = width // HEAD_DIM
    blocks = lax.axis_size("seq")
    peers = lax.axis_size("fsdp")
    sds, vmem = jax.ShapeDtypeStruct, pltpu.VMEM
    gain_row = gain.reshape(1, width)
    small = 2 * rows * width * HEAD_DIM
    big = 2 * rows * rows * width

    (state,) = call(
        state_kernel,
        [vmem((width, HEAD_DIM), F32)],
        small,
        key,
        value,
        scratch=[
            VMEM((rows, width), BF16),
            VMEM((rows, width), BF16),
            pltpu.SemaphoreType.DMA((2, 4)),
        ],
        homes=[HBM] * 2,
        spaces=[HBM] * 2,
    )
    slices = exchange(state, "seq", SEQ_FIRST, (ROWS, HEAD_DIM))
    (local,) = call(
        local_kernel,
        [vmem((rows, width), F32)],
        2 * big,
        query,
        key,
        value,
        homes=[HBM] * 3,
    )
    slices = slices.reshape(blocks, ROWS, HEAD_DIM)
    (slices,) = call(prefix_kernel, [vmem(slices.shape, F32)], width * HEAD_DIM, slices)
    prefix = exchange(slices.reshape(width, HEAD_DIM), "seq", SEQ_FIRST, (ROWS, HEAD_DIM))

    attended, stats = call(
        stats_kernel,
        [
            vmem((rows, width), F32),
            vmem((peers, 2 * rows // HEAD_DIM, HEAD_DIM), F32),
        ],
        small,
        query,
        local,
        prefix,
        cotangent,
        gain_row,
    )
    stats = exchange(stats, "fsdp", FSDP_FIRST, stats.shape[1:])
    grads, grad_state = call(
        grads_kernel,
        [vmem((rows, width), BF16), sds((blocks * GAIN_ROWS, HEAD_DIM), F32)],
        small,
        attended,
        cotangent,
        gain_row,
        stats,
        query,
    )
    grad_slices = exchange(grad_state, "seq", SEQ_FIRST, (GAIN_ROWS, 1, HEAD_DIM))
    query_grad, key_local, value_local = call(
        backward_kernel,
        [
            sds((rows, width), BF16),
            vmem((rows, width), F32),
            vmem((rows, width), F32),
        ],
        4 * big + small,
        query,
        key,
        value,
        grads,
        prefix,
        scratch=[VMEM((rows, rows), BF16), VMEM((rows, rows), BF16)],
        homes=[HBM] * 5,
    )
    (grad_slices,) = call(
        suffix_kernel, [vmem(grad_slices.shape, F32)], width * HEAD_DIM, grad_slices
    )
    suffix = exchange(grad_slices, "seq", SEQ_FIRST, (GAIN_ROWS, 1, HEAD_DIM))
    key_grad, value_grad, gain_grad = call(
        final_kernel,
        [
            sds((rows, width), BF16),
            sds((rows, width), BF16),
            sds((heads, HEAD_DIM), F32),
        ],
        2 * small,
        key_local,
        value_local,
        key,
        value,
        suffix,
    )
    return query_grad, key_grad, value_grad, gain_grad.reshape(width)


def solution(mesh):
    in_specs = (P("seq", "fsdp"), P("seq", "fsdp"), P("seq", "fsdp"), P("seq", "fsdp"), P("fsdp"))
    out_specs = (P("seq", "fsdp"), P("seq", "fsdp"), P("seq", "fsdp"), P("fsdp"))
    return jax.shard_map(shards, mesh=mesh, in_specs=in_specs, out_specs=out_specs, check_vma=False)
```
